32 devices in a mesh: tm: 4 (over y, x), space: 2 (over core), ens: 4 (over z).
Axes of the slice: x: 2, y: 2, z: 4, core: 2. Of those that a mesh axis runs over, the one named last changes fastest.
Arguments:
- initial_state: float32 [4, 4, 32, 512], P('ens', None, 'space'), may hold values from -6 to 6
- forcing: float32 [2, 32, 512], P(None, 'space'), may hold values from -6 to 6
- w_down: bfloat16 [128, 16], replicated, may hold values from -1.5 to 1.5
- depth_kernel: float32 [2, 128, 9], replicated, may hold values from -2 to 2
- w_point: bfloat16 [2, 128, 128], replicated, may hold values from -0.5 to 0.5
- w_up: bfloat16 [16, 128], replicated, may hold values from -0.25 to 0.25
Outputs:
- slice_ends: float32 [4, 4, 4, 32, 512], P('ens', 'tm', None, 'space')
- ensemble_mean: float32 [4, 4, 32, 512], P('tm', None, 'space')
The draws below stay inside these ranges and needn't reach their ends.
All inputs are finite; a program needn't handle non-finite values.
Results may differ from the reference program's by a relative error of at most 0.0084.
Values may be sent and summed in bfloat16 or wider, within the bound.
A program may use at most 64 MiB of HBM per device.

```python
import jax
import jax.numpy as jnp

FIELDS = 4
CH = 128
LAYERS = 2
ITERS = 2
FINE = 4
COLS = 512
NROWS = 32
SLICES = 4
MEMBERS = 4


def steps_of(own_key, shape, shards, least, top_value):
    loudness = 1.0
    for dim, shards_of in shards:
        steps = jax.random.uniform(jax.random.fold_in(jax.random.fold_in(own_key, 6), dim), (shards_of,), jnp.float32, least / len(shards), top_value / len(shards))
        loudness = loudness * jnp.repeat(jnp.exp(steps), shape[dim] // shards_of).reshape((-1,) + (1,) * (len(shape) - 1 - dim))
    return loudness


def normal_values(rng, dims, scale, reach, split=(), held_as=jnp.bfloat16):
    gain = steps_of(rng, dims, split, -0.22, 0.18) if split else 1.0
    array = jax.random.normal(rng, dims, jnp.float32) * scale * gain
    return jnp.minimum(jnp.maximum(array, -reach), reach).astype(held_as)


def setup_inputs(seed: int = 0) -> dict:
    splits = jax.random.split(jax.random.key(seed), 7)
    initial_state = normal_values(splits[0], (MEMBERS, FIELDS, NROWS, COLS), 1.0, 6.0, ((0, 4), (2, 2)), jnp.float32)
    forcing = normal_values(splits[1], (2, NROWS, COLS), 1.0, 6.0, ((1, 2),), jnp.float32)
    w_down = normal_values(splits[2], (CH, 4 * FIELDS), (4 * FIELDS) ** -0.5, 1.5)
    depth_kernel = normal_values(splits[3], (LAYERS, CH, 9), 9 ** -0.5, 2.0, (), jnp.float32)
    w_point = normal_values(splits[4], (LAYERS, CH, CH), CH ** -0.5, 0.5)
    w_up = normal_values(splits[5], (4 * FIELDS, CH), (4 * CH) ** -0.5, 0.25)
    return dict(initial_state=initial_state, forcing=forcing, w_down=w_down, depth_kernel=depth_kernel, w_point=w_point, w_up=w_up)


TIME_STEP = 0.05
VISCOSITY = 0.5
WAVE_SQ = 1.0
DIFFUSIVITY = 0.3


def advance(center, northern, southern, eastern, western, forcing):
    across = (eastern - western) * 0.5
    downward = (southern - northern) * 0.5
    laplace = northern + southern + eastern + western - 4.0 * center
    carried = center[0] * across + center[1] * downward
    rate_u = -carried[0] - across[2] + VISCOSITY * laplace[0] + forcing[0]
    rate_v = -carried[1] - downward[2] + VISCOSITY * laplace[1] + forcing[1]
    rate_p = -WAVE_SQ * (across[0] + downward[1]) + VISCOSITY * laplace[2]
    rate_s = -carried[3] + DIFFUSIVITY * laplace[3]
    return center + TIME_STEP * jnp.stack([rate_u, rate_v, rate_p, rate_s])


def fine_ref(state_in, forcing):
    for substep in range(FINE):
        state_in = advance(state_in, jnp.roll(state_in, 1, axis=1), jnp.roll(state_in, -1, axis=1),
                           jnp.roll(state_in, -1, axis=2), jnp.roll(state_in, 1, axis=2), forcing)
    return state_in


def to_patches(grid):
    fields, height, columns = grid.shape
    grouped = grid.reshape(fields, height // 2, 2, columns // 2, 2).transpose(0, 2, 4, 1, 3)
    return grouped.reshape(fields * 4, height // 2, columns // 2)


def from_patches(coarse_out, fields):
    height, columns = coarse_out.shape[1], coarse_out.shape[2]
    grouped = coarse_out.reshape(fields, 2, 2, height, columns).transpose(0, 3, 1, 4, 2)
    return grouped.reshape(fields, height * 2, columns * 2)


def depthwise_ref(hidden, kernel):
    summed = jnp.zeros(hidden.shape, jnp.float32)
    for offset_row in (-1, 0, 1):
        band = jnp.roll(hidden, -offset_row, axis=1).astype(jnp.float32)
        for offset_col in (-1, 0, 1):
            tap = kernel[:, (offset_row + 1) * 3 + offset_col + 1].astype(jnp.float32)
            summed = summed + tap[:, None, None] * jnp.roll(band, -offset_col, axis=2)
    return summed


def coarse_ref(state_in, w_down, depth_kernel, w_point, w_up):
    patches = to_patches(state_in.astype(jnp.bfloat16))
    hidden = jnp.einsum("cq,qrw->crw", w_down.astype(jnp.float32), patches.astype(jnp.float32)).astype(jnp.bfloat16)
    for depth_level in range(LAYERS):
        filtered = depthwise_ref(hidden, depth_kernel[depth_level]).astype(jnp.bfloat16)
        lifted = jnp.einsum("oc,crw->orw", w_point[depth_level].astype(jnp.float32), filtered.astype(jnp.float32))
        hidden = (hidden.astype(jnp.float32) + jax.nn.gelu(lifted)).astype(jnp.bfloat16)
    output = jnp.einsum("qc,crw->qrw", w_up.astype(jnp.float32), hidden.astype(jnp.float32))
    return state_in + from_patches(output, state_in.shape[0])


def reference(initial_state, forcing, w_down, depth_kernel, w_point, w_up):
    def coarse(state_in):
        return coarse_ref(state_in, w_down, depth_kernel, w_point, w_up)

    every_member = []
    for member in range(MEMBERS):
        anchor = initial_state[member]
        starts = [anchor]
        coarse_old = []
        for slice_index in range(SLICES - 1):
            predicted = coarse(starts[-1])
            coarse_old.append(predicted)
            starts.append(predicted)
        coarse_old.append(coarse(starts[-1]))
        endings = []
        for rounds in range(ITERS):
            corrections = [fine_ref(starts[slice_index], forcing) - coarse_old[slice_index] for slice_index in range(SLICES)]
            refreshed = [anchor]
            coarse_new = []
            for slice_index in range(SLICES - 1):
                predicted = coarse(refreshed[-1])
                coarse_new.append(predicted)
                refreshed.append(predicted + corrections[slice_index])
            coarse_new.append(coarse(refreshed[-1]))
            endings = [coarse_new[slice_index] + corrections[slice_index] for slice_index in range(SLICES)]
            starts, coarse_old = refreshed, coarse_new
        every_member.append(jnp.stack(endings))
    slice_ends = jnp.stack(every_member)
    ensemble_mean = jnp.sum(slice_ends, axis=0) / MEMBERS
    return slice_ends, ensemble_mean
```

```python
import jax
import jax.numpy as jnp
from jax import lax
from jax.experimental import pallas as pl
from jax.experimental.pallas import tpu as pltpu
from jax.sharding import PartitionSpec as P

TIME_STEP = 0.05
VISCOSITY = 0.5
DIFFUSIVITY = 0.3
FINE = 4
MESH = pl.DeviceIdType.MESH
F32 = jnp.float32
BF16 = jnp.bfloat16


def swap_order(p):
    return p + lax.div(p, 2) * (1 - 2 * lax.rem(p, 2))


def iota(shape, dim):
    return lax.broadcasted_iota(jnp.int32, shape, dim)


def split3(x):
    hi = x.astype(BF16)
    rest = x - hi.astype(F32)
    mid = rest.astype(BF16)
    low = (rest - mid.astype(F32)).astype(BF16)
    return jnp.concatenate([hi, mid, low], axis=0)


def exact_move(x, pick):
    rows = x.shape[0]
    y = jnp.dot(split3(x), pick, preferred_element_type=F32)
    return y[:rows] + y[rows : 2 * rows] + y[2 * rows :]


def fine_sweep(state, force):
    cur = state
    rows = cur.shape[1]
    fields = cur.shape[0] // 2
    for _ in range(FINE):
        north = pltpu.roll(cur, 1, 1)
        south = pltpu.roll(cur, rows - 1, 1)
        down = (south - north) * 0.5
        vert = south + north - 4.0 * cur
        out = [None] * (2 * fields)
        for b in (0, 1):
            across, lap = [], []
            for f in range(fields):
                ev, od = cur[2 * f], cur[2 * f + 1]
                cols = ev.shape[1]
                if b == 0:
                    east, west = od, pltpu.roll(od, 1, 1)
                else:
                    east, west = pltpu.roll(ev, cols - 1, 1), ev
                across.append((east - west) * 0.5)
                lap.append(vert[2 * f + b] + east + west)
            u, v = cur[b], cur[2 + b]

            def carried(f):
                return u * across[f] + v * down[2 * f + b]

            rates = [
                VISCOSITY * lap[0] - carried(0) - across[2] + force[b],
                VISCOSITY * lap[1] - carried(1) - down[4 + b] + force[2 + b],
                VISCOSITY * lap[2] - (across[0] + down[2 + b]),
                DIFFUSIVITY * lap[3] - carried(3),
            ]
            for f in range(fields):
                out[2 * f + b] = cur[2 * f + b] + TIME_STEP * rates[f]
        cur = jnp.stack(out)
    return cur


def gelu(x):
    return 0.5 * x * (1.0 + jnp.tanh(0.7978845608028654 * (x + 0.044715 * x * x * x)))


def kernel(tm, spaces, u_ref, f_ref, wd_ref, kt_ref, wp_ref, wu_ref, ends_ref,
           wdb, wub, wcs, snd0, nrt0, sth0, snd, nrt, sth, send_sem, recv_sem):
    t = lax.axis_index("tm")
    s = lax.axis_index("space")
    fields, half, columns = u_ref.shape
    cols = columns // 2
    block = half // tm
    ch = wd_ref.shape[0]
    layers = wp_ref.shape[0]
    groups = 2 * fields
    padded = 4 * block
    pos = swap_order(t)
    ring = s * tm + pos
    total = tm * spaces
    neighbours = []
    for step in (total - 1, 1):
        g = lax.rem(ring + step, total)
        neighbours.append({"tm": swap_order(lax.rem(g, tm)), "space": lax.div(g, tm)})
    to_north, to_south = neighbours

    def exchange(stage, src, from_north, from_south):
        copies = [
            pltpu.make_async_remote_copy(src, from_south, send_sem.at[stage, 0], recv_sem.at[stage, 0],
                                         device_id=to_north, device_id_type=MESH),
            pltpu.make_async_remote_copy(src, from_north, send_sem.at[stage, 1], recv_sem.at[stage, 1],
                                         device_id=to_south, device_id_type=MESH),
        ]
        for c in copies:
            c.start()
        return copies

    def own_rows(ref):
        picked = ref[:, 0:block, :]
        for k in range(1, tm):
            picked = jnp.where(pos == k, ref[:, k * block : (k + 1) * block, :], picked)
        return picked

    r_i, c_i = iota((columns, columns), 0), iota((columns, columns), 1)
    odd = jnp.where(c_i >= cols, 1, 0)
    to_parity = jnp.where(r_i == 2 * (c_i - odd * cols) + odd, 1.0, 0.0).astype(BF16)
    both = jnp.concatenate([own_rows(u_ref), own_rows(f_ref)], axis=0)
    count = fields + f_ref.shape[0]
    moved = exact_move(both.reshape(count * block, columns), to_parity).reshape(count, block, columns)
    for f in range(count):
        for b in (0, 1):
            snd0[2 * f + b] = moved[f, :, b * cols : (b + 1) * cols]
    copies = exchange(0, snd0, nrt0, sth0)

    rows_in = 3 * block // 2
    wide = groups * padded
    for r in range(rows_in):
        q, k = iota((2 * groups, wide), 0), iota((2 * groups, wide), 1)
        fq, aq, bq = q // 4, (q // 2) % 2, q % 2
        gk, rk = k // padded, k % padded
        sel = jnp.where((gk == 2 * fq + bq) & (rk == 2 * r + aq), 1.0, 0.0).astype(BF16)
        wdb[r * ch : (r + 1) * ch] = jnp.dot(wd_ref[...], sel, preferred_element_type=F32).astype(BF16)
    small = groups * block
    for r in range(block // 2):
        q, k = iota((small, 2 * groups), 1), iota((small, 2 * groups), 0)
        fq, aq, bq = q // 4, (q // 2) % 2, q % 2
        gk, rk = k // block, k % block
        sel = jnp.where((gk == 2 * fq + bq) & (rk == 2 * r + aq), 1.0, 0.0).astype(BF16)
        wub[:, r * ch : (r + 1) * ch] = jnp.dot(sel, wu_ref[...], preferred_element_type=F32).astype(BF16)
    for l in range(layers):
        w = wp_ref[l].astype(F32)
        for a in range(3):
            for b in range(3):
                tap = kt_ref[l, 3 * a + b : 3 * a + b + 1, :]
                wcs[l, b * ch : (b + 1) * ch, a * ch : (a + 1) * ch] = (w * tap).astype(BF16)

    def coarse(own, state):
        x = state.astype(BF16).reshape(wide, cols)
        hidden = jnp.dot(wdb[...], x, preferred_element_type=F32).astype(BF16)
        for l in range(layers):
            n_out = hidden.shape[0] // ch - 2
            new = []
            for r in range(n_out):
                y = jnp.dot(wcs[l], hidden[r * ch : (r + 3) * ch], preferred_element_type=F32)
                lifted = y[ch : 2 * ch] + pltpu.roll(y[:ch], 1, 1) + pltpu.roll(y[2 * ch :], cols - 1, 1)
                old = hidden[(r + 1) * ch : (r + 2) * ch].astype(F32)
                new.append((old + gelu(lifted)).astype(BF16))
            hidden = jnp.concatenate(new, axis=0)
        delta = jnp.dot(wub[...], hidden, preferred_element_type=F32)
        return own + delta.reshape(groups, block, cols)

    def fine(state):
        return fine_sweep(state, force)[:, block : 2 * block]

    def pad(north, own, south):
        return jnp.concatenate([north, own, south, jnp.zeros_like(own)], axis=1)

    r_j, c_j = iota((columns, columns), 0), iota((columns, columns), 1)
    odd_j = jnp.where(r_j >= cols, 1, 0)
    from_parity = jnp.where(c_j == 2 * (r_j - odd_j * cols) + odd_j, 1.0, 0.0).astype(BF16)

    def finish(n, end):
        pieces = [jnp.concatenate([end[2 * f], end[2 * f + 1]], axis=1) for f in range(fields)]
        flat = jnp.concatenate(pieces, axis=0)
        ends_ref[n] = exact_move(flat, from_parity).reshape(fields, block, columns)

    def next_stage(stage, starts):
        for i, start in enumerate(starts):
            snd[stage - 1, i] = start
        k = len(starts)
        return exchange(stage, snd.at[stage - 1, 0:k], nrt.at[stage - 1, 0:k], sth.at[stage - 1, 0:k])

    def arrived(stage, moving, starts):
        for c in moving:
            c.wait()
        return [pad(nrt[stage - 1, i], start, sth[stage - 1, i]) for i, start in enumerate(starts)]

    for c in copies:
        c.wait()
    everything = pad(nrt0[...], snd0[...], sth0[...])
    force = everything[groups:]
    start0 = snd0[0:groups]
    state0 = everything[:groups]

    g0 = coarse(start0, state0)
    v1 = g0 + (fine(state0) - g0)
    u1 = g0
    moving = next_stage(1, [u1, v1])
    finish(0, v1)
    u1p, v1p = arrived(1, moving, [u1, v1])

    u2 = coarse(u1, u1p)
    gv1 = coarse(v1, v1p)
    v2 = gv1 + (fine(u1p) - u2)
    w2 = gv1 + (fine(v1p) - gv1)
    moving = next_stage(2, [u2, v2, w2])
    finish(1, w2)
    u2p, v2p, w2p = arrived(2, moving, [u2, v2, w2])

    gu2 = coarse(u2, u2p)
    gv2 = coarse(v2, v2p)
    gw2 = coarse(w2, w2p)
    v3 = gv2 + (fine(u2p) - gu2)
    w3 = gw2 + (fine(v2p) - gv2)
    moving = next_stage(3, [v3, w3])
    finish(2, w3)
    v3p, w3p = arrived(3, moving, [v3, w3])

    gv3 = coarse(v3, v3p)
    gw3 = coarse(w3, w3p)
    finish(3, gw3 + (fine(v3p) - gv3))


def local(initial_state, forcing, w_down, depth_kernel, w_point, w_up):
    tm, spaces = lax.axis_size("tm"), lax.axis_size("space")
    _, fields, half, columns = initial_state.shape
    block = half // tm
    cols, groups = columns // 2, 2 * fields
    layers, ch, _ = depth_kernel.shape
    assert block == FINE == 2 * layers and tm == 4
    taps = jnp.swapaxes(depth_kernel, 1, 2)
    count = groups + 2 * forcing.shape[0]
    vmem = pl.BlockSpec(memory_space=pltpu.VMEM)
    ends = pl.pallas_call(
        lambda *refs: kernel(tm, spaces, *refs),
        name="parareal",
        out_shape=jax.ShapeDtypeStruct((tm, fields, block, columns), F32),
        in_specs=[vmem] * 6,
        out_specs=vmem,
        scratch_shapes=[
            pltpu.VMEM((3 * block // 2 * ch, groups * 4 * block), BF16),
            pltpu.VMEM((groups * block, block // 2 * ch), BF16),
            pltpu.VMEM((layers, 3 * ch, 3 * ch), BF16),
            pltpu.VMEM((count, block, cols), F32),
            pltpu.VMEM((count, block, cols), F32),
            pltpu.VMEM((count, block, cols), F32),
            pltpu.VMEM((3, 3, groups, block, cols), F32),
            pltpu.VMEM((3, 3, groups, block, cols), F32),
            pltpu.VMEM((3, 3, groups, block, cols), F32),
            pltpu.SemaphoreType.DMA((4, 2)),
            pltpu.SemaphoreType.DMA((4, 2)),
        ],
        compiler_params=pltpu.CompilerParams(has_side_effects=True, vmem_limit_bytes=32 << 20),
    )(initial_state[0], forcing, w_down, taps, w_point, w_up)
    gathered = lax.all_to_all(ends, "tm", 0, 0)
    order = jnp.stack([gathered[p] for p in (0, 1, 3, 2)], axis=1)
    ending = order.reshape(fields, half, columns)
    mean = lax.psum(ending, "ens") / lax.axis_size("ens")
    return ending[None, None], mean[None]


def solution(mesh):
    in_specs = (P("ens", None, "space", None), P(None, "space", None), P(), P(), P(), P())
    out_specs = (P("ens", "tm", None, "space", None), P("tm", None, "space", None))
    return jax.shard_map(local, mesh=mesh, in_specs=in_specs, out_specs=out_specs, check_vma=False)
```

```python
import jax
import jax.numpy as jnp
from jax import lax
from jax.experimental import pallas as pl
from jax.experimental.pallas import tpu as pltpu
from jax.sharding import PartitionSpec as P

TIME_STEP = 0.05
VISCOSITY = 0.5
DIFFUSIVITY = 0.3
FINE = 4
MESH = pl.DeviceIdType.MESH
F32 = jnp.float32
BF16 = jnp.bfloat16


def swap_order(p):
    if isinstance(p, int):
        return p + (p // 2) * (1 - 2 * (p % 2))
    return p + lax.div(p, 2) * (1 - 2 * lax.rem(p, 2))


def iota(shape, dim):
    return lax.broadcasted_iota(jnp.int32, shape, dim)


def split3(x):
    hi = x.astype(BF16)
    rest = x - hi.astype(F32)
    mid = rest.astype(BF16)
    low = (rest - mid.astype(F32)).astype(BF16)
    return jnp.concatenate([hi, mid, low], axis=0)


def exact_move(x, pick):
    rows = x.shape[0]
    y = jnp.dot(split3(x), pick, preferred_element_type=F32)
    return y[:rows] + y[rows : 2 * rows] + y[2 * rows :]


def fine_sweep(state, force):
    cur = state
    rows = cur.shape[1]
    fields = cur.shape[0] // 2
    for _ in range(FINE):
        north = pltpu.roll(cur, 1, 1)
        south = pltpu.roll(cur, rows - 1, 1)
        down = (south - north) * 0.5
        vert = south + north - 4.0 * cur
        out = [None] * (2 * fields)
        for b in (0, 1):
            across, lap = [], []
            for f in range(fields):
                ev, od = cur[2 * f], cur[2 * f + 1]
                cols = ev.shape[1]
                if b == 0:
                    east, west = od, pltpu.roll(od, 1, 1)
                else:
                    east, west = pltpu.roll(ev, cols - 1, 1), ev
                across.append((east - west) * 0.5)
                lap.append(vert[2 * f + b] + east + west)
            u, v = cur[b], cur[2 + b]

            def carried(f):
                return u * across[f] + v * down[2 * f + b]

            rates = [
                VISCOSITY * lap[0] - carried(0) - across[2] + force[b],
                VISCOSITY * lap[1] - carried(1) - down[4 + b] + force[2 + b],
                VISCOSITY * lap[2] - (across[0] + down[2 + b]),
                DIFFUSIVITY * lap[3] - carried(3),
            ]
            for f in range(fields):
                out[2 * f + b] = cur[2 * f + b] + TIME_STEP * rates[f]
        cur = jnp.stack(out)
    return cur


def gelu(x):
    return 0.5 * x * (1.0 + jnp.tanh(0.7978845608028654 * (x + 0.044715 * x * x * x)))


def kernel(tm, spaces, ens, u_hbm, f_hbm, wd_hbm, dk_hbm, wp_hbm, wu_hbm, out_ref, mean_ref,
           u_in, f_in, wd_ref, dk_ref, wp_ref, wu_ref,
           wdb, wub, wcs, snd0, nrt0, sth0, snd, nrt, sth,
           ebuf, parts, mbuf, got, got_mean,
           load_sem, send_sem, recv_sem, end_send, end_recv, part_send, part_recv, mean_send, mean_recv):
    loads = []
    for i, (src, dst) in enumerate([(u_hbm, u_in), (f_hbm, f_in), (wd_hbm, wd_ref), (dk_hbm, dk_ref),
                                    (wp_hbm, wp_ref), (wu_hbm, wu_ref)]):
        loads.append(pltpu.make_async_copy(src, dst, load_sem.at[i]))
    for c in loads:
        c.start()
    u_ref, f_ref = u_in.at[0], f_in
    e = lax.axis_index("ens")
    t = lax.axis_index("tm")
    s = lax.axis_index("space")
    fields, half, columns = u_ref.shape
    cols = columns // 2
    block = half // tm
    ch = wd_ref.shape[0]
    layers = wp_ref.shape[0]
    groups = 2 * fields
    padded = 4 * block
    pos = swap_order(t)
    ring = s * tm + pos
    total = tm * spaces
    neighbours = []
    for step in (total - 1, 1):
        g = lax.rem(ring + step, total)
        neighbours.append({"tm": swap_order(lax.rem(g, tm)), "space": lax.div(g, tm)})
    to_north, to_south = neighbours

    def exchange(stage, src, from_north, from_south):
        copies = [
            pltpu.make_async_remote_copy(src, from_south, send_sem.at[stage, 0], recv_sem.at[stage, 0],
                                         device_id=to_north, device_id_type=MESH),
            pltpu.make_async_remote_copy(src, from_north, send_sem.at[stage, 1], recv_sem.at[stage, 1],
                                         device_id=to_south, device_id_type=MESH),
        ]
        for c in copies:
            c.start()
        return copies

    def own_rows(ref):
        picked = ref[:, 0:block, :]
        for k in range(1, tm):
            picked = jnp.where(pos == k, ref[:, k * block : (k + 1) * block, :], picked)
        return picked

    loads[0].wait()
    loads[1].wait()
    r_i, c_i = iota((columns, columns), 0), iota((columns, columns), 1)
    odd = jnp.where(c_i >= cols, 1, 0)
    to_parity = jnp.where(r_i == 2 * (c_i - odd * cols) + odd, 1.0, 0.0).astype(BF16)
    both = jnp.concatenate([own_rows(u_ref), own_rows(f_ref)], axis=0)
    count = fields + f_ref.shape[0]
    moved = exact_move(both.reshape(count * block, columns), to_parity).reshape(count, block, columns)
    for f in range(count):
        for b in (0, 1):
            snd0[2 * f + b] = moved[f, :, b * cols : (b + 1) * cols]
    copies = exchange(0, snd0, nrt0, sth0)

    for c in loads[2:]:
        c.wait()
    rows_in = 3 * block // 2
    wide = groups * padded
    for r in range(rows_in):
        q, k = iota((2 * groups, wide), 0), iota((2 * groups, wide), 1)
        fq, aq, bq = q // 4, (q // 2) % 2, q % 2
        gk, rk = k // padded, k % padded
        sel = jnp.where((gk == 2 * fq + bq) & (rk == 2 * r + aq), 1.0, 0.0).astype(BF16)
        wdb[r * ch : (r + 1) * ch] = jnp.dot(wd_ref[...], sel, preferred_element_type=F32).astype(BF16)
    small = groups * block
    for r in range(block // 2):
        q, k = iota((small, 2 * groups), 1), iota((small, 2 * groups), 0)
        fq, aq, bq = q // 4, (q // 2) % 2, q % 2
        gk, rk = k // block, k % block
        sel = jnp.where((gk == 2 * fq + bq) & (rk == 2 * r + aq), 1.0, 0.0).astype(BF16)
        wub[:, r * ch : (r + 1) * ch] = jnp.dot(sel, wu_ref[...], preferred_element_type=F32).astype(BF16)
    for l in range(layers):
        w = wp_ref[l].astype(F32)
        taps = dk_ref[l].T
        for a in range(3):
            for b in range(3):
                tap = taps[3 * a + b : 3 * a + b + 1, :]
                wcs[l, b * ch : (b + 1) * ch, a * ch : (a + 1) * ch] = (w * tap).astype(BF16)

    def coarse(own, state):
        x = state.astype(BF16).reshape(wide, cols)
        hidden = jnp.dot(wdb[...], x, preferred_element_type=F32).astype(BF16)
        for l in range(layers):
            n_out = hidden.shape[0] // ch - 2
            new = []
            for r in range(n_out):
                y = jnp.dot(wcs[l], hidden[r * ch : (r + 3) * ch], preferred_element_type=F32)
                lifted = y[ch : 2 * ch] + pltpu.roll(y[:ch], 1, 1) + pltpu.roll(y[2 * ch :], cols - 1, 1)
                old = hidden[(r + 1) * ch : (r + 2) * ch].astype(F32)
                new.append((old + gelu(lifted)).astype(BF16))
            hidden = jnp.concatenate(new, axis=0)
        delta = jnp.dot(wub[...], hidden, preferred_element_type=F32)
        return own + delta.reshape(groups, block, cols)

    def fine(state):
        return fine_sweep(state, force)[:, block : 2 * block]

    def pad(north, own, south):
        return jnp.concatenate([north, own, south, jnp.zeros_like(own)], axis=1)

    r_j, c_j = iota((columns, columns), 0), iota((columns, columns), 1)
    odd_j = jnp.where(r_j >= cols, 1, 0)
    from_parity = jnp.where(c_j == 2 * (r_j - odd_j * cols) + odd_j, 1.0, 0.0).astype(BF16)

    chunk = fields // ens

    def finish(n, end):
        pieces = [jnp.concatenate([end[2 * f], end[2 * f + 1]], axis=1) for f in range(fields)]
        flat = jnp.concatenate(pieces, axis=0)
        ebuf[n] = exact_move(flat, from_parity).reshape(fields, block, columns)
        for d in range(1, ens):
            part_copy(n, d).start()

        @pl.when(t != n)
        def _():
            end_copy(n).start()

    def part_copy(n, d):
        other = lax.rem(e + d, ens)
        return pltpu.make_async_remote_copy(
            ebuf.at[n, pl.ds(other * chunk, chunk)], parts.at[n, d - 1], part_send.at[n, d - 1], part_recv.at[n, d - 1],
            device_id={"ens": other}, device_id_type=MESH)

    def end_copy(n):
        return pltpu.make_async_remote_copy(
            ebuf.at[n], got.at[pos], end_send.at[n], end_recv.at[t],
            device_id={"tm": n}, device_id_type=MESH)

    def mean_copy(n, d):
        return pltpu.make_async_remote_copy(
            mbuf.at[n], got_mean.at[pos, d], mean_send.at[n, d], mean_recv.at[t, d],
            device_id={"tm": n, "ens": lax.rem(e + d, ens)}, device_id_type=MESH)

    def reduce(n):
        acc = ebuf[n, pl.ds(e * chunk, chunk)]
        for d in range(1, ens):
            part_copy(n, d).wait()
            acc = acc + parts[n, d - 1]
        mbuf[n] = acc * (1.0 / ens)
        for d in range(1, ens):
            mean_copy(n, d).start()

        @pl.when(t != n)
        def _():
            mean_copy(n, 0).start()

    def collect():
        for n in range(tm):
            @pl.when(t != n)
            def _():
                end_copy(n).wait_send()
                mean_copy(n, 0).wait_send()
                pltpu.make_async_remote_copy(
                    ebuf.at[n], got.at[swap_order(n)], end_send.at[n], end_recv.at[n],
                    device_id={"tm": n}, device_id_type=MESH).wait_recv()
                pltpu.make_async_remote_copy(
                    mbuf.at[n], got_mean.at[swap_order(n), 0], mean_send.at[n, 0], mean_recv.at[n, 0],
                    device_id={"tm": n}, device_id_type=MESH).wait_recv()

            @pl.when(t == n)
            def _():
                got[swap_order(n)] = ebuf[n]
                got_mean[swap_order(n), 0] = mbuf[n]

            for d in range(1, ens):
                mean_copy(n, d).wait_send()
                pltpu.make_async_remote_copy(
                    mbuf.at[n], got_mean.at[swap_order(n), d], mean_send.at[n, d], mean_recv.at[n, d],
                    device_id={"ens": lax.rem(e + d, ens)}, device_id_type=MESH).wait_recv()
        for p in range(tm):
            out_ref[:, p * block : (p + 1) * block, :] = got[p]
            for d in range(ens):
                first = lax.rem(e + ens - d, ens) * chunk
                mean_ref[pl.ds(first, chunk), p * block : (p + 1) * block, :] = got_mean[p, d]

    def next_stage(stage, starts):
        for i, start in enumerate(starts):
            snd[stage - 1, i] = start
        k = len(starts)
        return exchange(stage, snd.at[stage - 1, 0:k], nrt.at[stage - 1, 0:k], sth.at[stage - 1, 0:k])

    def arrived(stage, moving, starts):
        for c in moving:
            c.wait()
        return [pad(nrt[stage - 1, i], start, sth[stage - 1, i]) for i, start in enumerate(starts)]

    for c in copies:
        c.wait()
    everything = pad(nrt0[...], snd0[...], sth0[...])
    force = everything[groups:]
    start0 = snd0[0:groups]
    state0 = everything[:groups]

    g0 = coarse(start0, state0)
    v1 = g0 + (fine(state0) - g0)
    u1 = g0
    moving = next_stage(1, [u1, v1])
    finish(0, v1)
    u1p, v1p = arrived(1, moving, [u1, v1])

    u2 = coarse(u1, u1p)
    gv1 = coarse(v1, v1p)
    v2 = gv1 + (fine(u1p) - u2)
    w2 = gv1 + (fine(v1p) - gv1)
    moving = next_stage(2, [u2, v2, w2])
    finish(1, w2)
    reduce(0)
    u2p, v2p, w2p = arrived(2, moving, [u2, v2, w2])

    gu2 = coarse(u2, u2p)
    gv2 = coarse(v2, v2p)
    gw2 = coarse(w2, w2p)
    v3 = gv2 + (fine(u2p) - gu2)
    w3 = gw2 + (fine(v2p) - gv2)
    moving = next_stage(3, [v3, w3])
    finish(2, w3)
    reduce(1)
    v3p, w3p = arrived(3, moving, [v3, w3])

    gv3 = coarse(v3, v3p)
    gw3 = coarse(w3, w3p)
    finish(3, gw3 + (fine(v3p) - gv3))
    reduce(2)
    reduce(3)
    collect()


def local(initial_state, forcing, w_down, depth_kernel, w_point, w_up):
    tm, spaces, ens = lax.axis_size("tm"), lax.axis_size("space"), lax.axis_size("ens")
    _, fields, half, columns = initial_state.shape
    block = half // tm
    cols, groups = columns // 2, 2 * fields
    layers, ch, _ = depth_kernel.shape
    assert block == FINE == 2 * layers and tm == 4
    assert fields % ens == 0
    count = groups + 2 * forcing.shape[0]
    chunk = fields // ens
    vmem = pl.BlockSpec(memory_space=pltpu.VMEM)
    hbm = pl.BlockSpec(memory_space=pl.ANY)
    args = (initial_state, forcing, w_down, depth_kernel, w_point, w_up)
    ending, mean = pl.pallas_call(
        lambda *refs: kernel(tm, spaces, ens, *refs),
        name="parareal",
        out_shape=[jax.ShapeDtypeStruct((fields, half, columns), F32)] * 2,
        in_specs=[hbm] * 6,
        out_specs=[vmem] * 2,
        scratch_shapes=[pltpu.VMEM(a.shape, a.dtype) for a in args] + [
            pltpu.VMEM((3 * block // 2 * ch, groups * 4 * block), BF16),
            pltpu.VMEM((groups * block, block // 2 * ch), BF16),
            pltpu.VMEM((layers, 3 * ch, 3 * ch), BF16),
            pltpu.VMEM((count, block, cols), F32),
            pltpu.VMEM((count, block, cols), F32),
            pltpu.VMEM((count, block, cols), F32),
            pltpu.VMEM((3, 3, groups, block, cols), F32),
            pltpu.VMEM((3, 3, groups, block, cols), F32),
            pltpu.VMEM((3, 3, groups, block, cols), F32),
            pltpu.VMEM((tm, fields, block, columns), F32),
            pltpu.VMEM((tm, max(ens - 1, 1), chunk, block, columns), F32),
            pltpu.VMEM((tm, chunk, block, columns), F32),
            pltpu.VMEM((tm, fields, block, columns), F32),
            pltpu.VMEM((tm, ens, chunk, block, columns), F32),
            pltpu.SemaphoreType.DMA((6,)),
            pltpu.SemaphoreType.DMA((4, 2)),
            pltpu.SemaphoreType.DMA((4, 2)),
            pltpu.SemaphoreType.DMA((tm,)),
            pltpu.SemaphoreType.DMA((tm,)),
            pltpu.SemaphoreType.DMA((tm, max(ens - 1, 1))),
            pltpu.SemaphoreType.DMA((tm, max(ens - 1, 1))),
            pltpu.SemaphoreType.DMA((tm, ens)),
            pltpu.SemaphoreType.DMA((tm, ens)),
        ],
        compiler_params=pltpu.CompilerParams(has_side_effects=True, vmem_limit_bytes=32 << 20),
    )(*args)
    return ending[None, None], mean[None]


def solution(mesh):
    in_specs = (P("ens", None, "space", None), P(None, "space", None), P(), P(), P(), P())
    out_specs = (P("ens", "tm", None, "space", None), P("tm", None, "space", None))
    return jax.shard_map(local, mesh=mesh, in_specs=in_specs, out_specs=out_specs, check_vma=False)
```

```python
import jax
import jax.numpy as jnp
from jax import lax
from jax.experimental import pallas as pl
from jax.experimental.pallas import tpu as pltpu
from jax.sharding import PartitionSpec as P

TIME_STEP = 0.05
VISCOSITY = 0.5
DIFFUSIVITY = 0.3
FINE = 4
MESH = pl.DeviceIdType.MESH
F32 = jnp.float32
BF16 = jnp.bfloat16


def swap_order(p):
    if isinstance(p, int):
        return p + (p // 2) * (1 - 2 * (p % 2))
    return p + lax.div(p, 2) * (1 - 2 * lax.rem(p, 2))


def iota(shape, dim):
    return lax.broadcasted_iota(jnp.int32, shape, dim)


def split3(x):
    hi = x.astype(BF16)
    rest = x - hi.astype(F32)
    mid = rest.astype(BF16)
    low = (rest - mid.astype(F32)).astype(BF16)
    return jnp.concatenate([hi, mid, low], axis=0)


def exact_move(x, pick):
    rows = x.shape[0]
    y = jnp.dot(split3(x), pick, preferred_element_type=F32)
    return y[:rows] + y[rows : 2 * rows] + y[2 * rows :]


def fine_sweep(state, force):
    cur = state
    rows = cur.shape[1]
    fields = cur.shape[0] // 2
    for _ in range(FINE):
        north = pltpu.roll(cur, 1, 1)
        south = pltpu.roll(cur, rows - 1, 1)
        down = (south - north) * 0.5
        vert = south + north - 4.0 * cur
        out = [None] * (2 * fields)
        for b in (0, 1):
            across, lap = [], []
            for f in range(fields):
                ev, od = cur[2 * f], cur[2 * f + 1]
                cols = ev.shape[1]
                if b == 0:
                    east, west = od, pltpu.roll(od, 1, 1)
                else:
                    east, west = pltpu.roll(ev, cols - 1, 1), ev
                across.append((east - west) * 0.5)
                lap.append(vert[2 * f + b] + east + west)
            u, v = cur[b], cur[2 + b]

            def carried(f):
                return u * across[f] + v * down[2 * f + b]

            rates = [
                VISCOSITY * lap[0] - carried(0) - across[2] + force[b],
                VISCOSITY * lap[1] - carried(1) - down[4 + b] + force[2 + b],
                VISCOSITY * lap[2] - (across[0] + down[2 + b]),
                DIFFUSIVITY * lap[3] - carried(3),
            ]
            for f in range(fields):
                out[2 * f + b] = cur[2 * f + b] + TIME_STEP * rates[f]
        cur = jnp.stack(out)
    return cur


def gelu(x):
    return 0.5 * x * (1.0 + jnp.tanh(0.7978845608028654 * (x + 0.044715 * x * x * x)))


def kernel(tm, spaces, ens, u_hbm, f_hbm, wd_hbm, dk_hbm, wp_hbm, wu_hbm, out_ref, mean_ref,
           u_in, f_in, wd_ref, dk_ref, wp_ref, wu_ref,
           wdb, wub, wcs, snd0, nrt0, sth0, snd, nrt, sth,
           ebuf, parts, mbuf, got, got_mean,
           load_sem, send_sem, recv_sem, end_send, end_recv, part_send, part_recv, mean_send, mean_recv):
    loads = []
    for i, (src, dst) in enumerate([(u_hbm, u_in), (f_hbm, f_in), (wd_hbm, wd_ref), (dk_hbm, dk_ref),
                                    (wp_hbm, wp_ref), (wu_hbm, wu_ref)]):
        loads.append(pltpu.make_async_copy(src, dst, load_sem.at[i]))
    for c in loads:
        c.start()
    u_ref, f_ref = u_in.at[0], f_in
    e = lax.axis_index("ens")
    t = lax.axis_index("tm")
    s = lax.axis_index("space")
    fields, half, columns = u_ref.shape
    cols = columns // 2
    block = half // tm
    ch = wd_ref.shape[0]
    layers = wp_ref.shape[0]
    groups = 2 * fields
    padded = 4 * block
    pos = swap_order(t)
    ring = s * tm + pos
    total = tm * spaces
    neighbours = []
    for step in (total - 1, 1):
        g = lax.rem(ring + step, total)
        neighbours.append({"tm": swap_order(lax.rem(g, tm)), "space": lax.div(g, tm)})
    to_north, to_south = neighbours

    def exchange(stage, src, from_north, from_south):
        copies = [
            pltpu.make_async_remote_copy(src, from_south, send_sem.at[stage, 0], recv_sem.at[stage, 0],
                                         device_id=to_north, device_id_type=MESH),
            pltpu.make_async_remote_copy(src, from_north, send_sem.at[stage, 1], recv_sem.at[stage, 1],
                                         device_id=to_south, device_id_type=MESH),
        ]
        for c in copies:
            c.start()
        return copies

    def own_rows(ref):
        picked = ref[:, 0:block, :]
        for k in range(1, tm):
            picked = jnp.where(pos == k, ref[:, k * block : (k + 1) * block, :], picked)
        return picked

    barrier = pltpu.get_barrier_semaphore()
    peers = neighbours + [{"tm": lax.rem(t + i, tm), "ens": lax.rem(e + j, ens)}
                          for i in range(tm) for j in range(ens) if i + j > 0]
    for peer in peers:
        pl.semaphore_signal(barrier, inc=1, device_id=peer, device_id_type=MESH)
    loads[0].wait()
    loads[1].wait()
    r_i, c_i = iota((columns, columns), 0), iota((columns, columns), 1)
    odd = jnp.where(c_i >= cols, 1, 0)
    to_parity = jnp.where(r_i == 2 * (c_i - odd * cols) + odd, 1.0, 0.0).astype(BF16)
    both = jnp.concatenate([own_rows(u_ref), own_rows(f_ref)], axis=0)
    count = fields + f_ref.shape[0]
    moved = exact_move(both.reshape(count * block, columns), to_parity).reshape(count, block, columns)
    first = []
    for f in range(count):
        for b in (0, 1):
            first.append(moved[f, :, b * cols : (b + 1) * cols])
    first = jnp.stack(first)
    snd0[...] = first.reshape(2 * count * block, cols).astype(snd0.dtype)
    pl.semaphore_wait(barrier, len(peers))
    copies = exchange(0, snd0, nrt0, sth0)

    for c in loads[2:]:
        c.wait()
    rows_in = 3 * block // 2
    wide = groups * padded
    for r in range(rows_in):
        q, k = iota((2 * groups, wide), 0), iota((2 * groups, wide), 1)
        fq, aq, bq = q // 4, (q // 2) % 2, q % 2
        gk, rk = k // padded, k % padded
        sel = jnp.where((gk == 2 * fq + bq) & (rk == 2 * r + aq), 1.0, 0.0).astype(BF16)
        wdb[r * ch : (r + 1) * ch] = jnp.dot(wd_ref[...], sel, preferred_element_type=F32).astype(BF16)
    small = groups * block
    for r in range(block // 2):
        q, k = iota((small, 2 * groups), 1), iota((small, 2 * groups), 0)
        fq, aq, bq = q // 4, (q // 2) % 2, q % 2
        gk, rk = k // block, k % block
        sel = jnp.where((gk == 2 * fq + bq) & (rk == 2 * r + aq), 1.0, 0.0).astype(BF16)
        wub[:, r * ch : (r + 1) * ch] = jnp.dot(sel, wu_ref[...], preferred_element_type=F32).astype(BF16)
    for l in range(layers):
        w = wp_ref[l].astype(F32)
        taps = dk_ref[l].T
        for a in range(3):
            for b in range(3):
                tap = taps[3 * a + b : 3 * a + b + 1, :]
                wcs[l, b * ch : (b + 1) * ch, a * ch : (a + 1) * ch] = (w * tap).astype(BF16)

    def coarse(own, state):
        x = state.astype(BF16).reshape(wide, cols)
        hidden = jnp.dot(wdb[...], x, preferred_element_type=F32).astype(BF16)
        for l in range(layers):
            n_out = hidden.shape[0] // ch - 2
            new = []
            for r in range(n_out):
                y = jnp.dot(wcs[l], hidden[r * ch : (r + 3) * ch], preferred_element_type=F32)
                lifted = y[ch : 2 * ch] + pltpu.roll(y[:ch], 1, 1) + pltpu.roll(y[2 * ch :], cols - 1, 1)
                old = hidden[(r + 1) * ch : (r + 2) * ch].astype(F32)
                new.append((old + gelu(lifted)).astype(BF16))
            hidden = jnp.concatenate(new, axis=0)
        delta = jnp.dot(wub[...], hidden, preferred_element_type=F32)
        return own + delta.reshape(groups, block, cols)

    def fine(state):
        return fine_sweep(state, force)[:, block : 2 * block]

    def unpack(x):
        return x.astype(F32).reshape(-1, block, cols)

    def pad(north, own, south):
        return jnp.concatenate([north, own, south, jnp.zeros_like(own)], axis=1)

    r_j, c_j = iota((columns, columns), 0), iota((columns, columns), 1)
    odd_j = jnp.where(r_j >= cols, 1, 0)
    from_parity = jnp.where(c_j == 2 * (r_j - odd_j * cols) + odd_j, 1.0, 0.0).astype(BF16)

    chunk = fields // ens

    def finish(n, end):
        pieces = [jnp.concatenate([end[2 * f], end[2 * f + 1]], axis=1) for f in range(fields)]
        flat = jnp.concatenate(pieces, axis=0)
        ebuf[n] = exact_move(flat, from_parity).reshape(fields, block, columns)
        for d in range(1, ens):
            part_copy(n, d).start()

        @pl.when(t != n)
        def _():
            end_copy(n).start()

    def part_copy(n, d):
        other = lax.rem(e + d, ens)
        return pltpu.make_async_remote_copy(
            ebuf.at[n, pl.ds(other * chunk, chunk)], parts.at[n, d - 1], part_send.at[n, d - 1], part_recv.at[n, d - 1],
            device_id={"ens": other}, device_id_type=MESH)

    def end_copy(n):
        return pltpu.make_async_remote_copy(
            ebuf.at[n], got.at[pos], end_send.at[n], end_recv.at[t],
            device_id={"tm": n}, device_id_type=MESH)

    def mean_copy(n, d):
        return pltpu.make_async_remote_copy(
            mbuf.at[n], got_mean.at[pos, d], mean_send.at[n, d], mean_recv.at[t, d],
            device_id={"tm": n, "ens": lax.rem(e + d, ens)}, device_id_type=MESH)

    def reduce(n):
        acc = ebuf[n, pl.ds(e * chunk, chunk)]
        for d in range(1, ens):
            part_copy(n, d).wait()
            acc = acc + parts[n, d - 1]
        mbuf[n] = acc * (1.0 / ens)
        for d in range(1, ens):
            mean_copy(n, d).start()

        @pl.when(t != n)
        def _():
            mean_copy(n, 0).start()

    def collect():
        for n in range(tm):
            @pl.when(t != n)
            def _():
                end_copy(n).wait_send()
                mean_copy(n, 0).wait_send()
                pltpu.make_async_remote_copy(
                    ebuf.at[n], got.at[swap_order(n)], end_send.at[n], end_recv.at[n],
                    device_id={"tm": n}, device_id_type=MESH).wait_recv()
                pltpu.make_async_remote_copy(
                    mbuf.at[n], got_mean.at[swap_order(n), 0], mean_send.at[n, 0], mean_recv.at[n, 0],
                    device_id={"tm": n}, device_id_type=MESH).wait_recv()

            @pl.when(t == n)
            def _():
                got[swap_order(n)] = ebuf[n]
                got_mean[swap_order(n), 0] = mbuf[n]

            for d in range(1, ens):
                mean_copy(n, d).wait_send()
                pltpu.make_async_remote_copy(
                    mbuf.at[n], got_mean.at[swap_order(n), d], mean_send.at[n, d], mean_recv.at[n, d],
                    device_id={"ens": lax.rem(e + d, ens)}, device_id_type=MESH).wait_recv()
        for p in range(tm):
            out_ref[:, p * block : (p + 1) * block, :] = got[p]
            for d in range(ens):
                first = lax.rem(e + ens - d, ens) * chunk
                mean_ref[pl.ds(first, chunk), p * block : (p + 1) * block, :] = got_mean[p, d]

    def next_stage(stage, starts):
        for i, start in enumerate(starts):
            snd[stage - 1, i] = start.reshape(groups * block, cols).astype(snd.dtype)
        k = len(starts)
        return exchange(stage, snd.at[stage - 1, 0:k], nrt.at[stage - 1, 0:k], sth.at[stage - 1, 0:k])

    def arrived(stage, moving, starts):
        for c in moving:
            c.wait()
        return [pad(unpack(nrt[stage - 1, i]), start, unpack(sth[stage - 1, i])) for i, start in enumerate(starts)]

    for c in copies:
        c.wait()
    everything = pad(unpack(nrt0[...]), first, unpack(sth0[...]))
    force = everything[groups:]
    start0 = first[:groups]
    state0 = everything[:groups]

    g0 = coarse(start0, state0)
    v1 = g0 + (fine(state0) - g0)
    u1 = g0
    moving = next_stage(1, [u1, v1])
    finish(0, v1)
    u1p, v1p = arrived(1, moving, [u1, v1])

    u2 = coarse(u1, u1p)
    gv1 = coarse(v1, v1p)
    v2 = gv1 + (fine(u1p) - u2)
    w2 = gv1 + (fine(v1p) - gv1)
    moving = next_stage(2, [u2, v2, w2])
    finish(1, w2)
    reduce(0)
    u2p, v2p, w2p = arrived(2, moving, [u2, v2, w2])

    gu2 = coarse(u2, u2p)
    gv2 = coarse(v2, v2p)
    gw2 = coarse(w2, w2p)
    v3 = gv2 + (fine(u2p) - gu2)
    w3 = gw2 + (fine(v2p) - gv2)
    moving = next_stage(3, [v3, w3])
    finish(2, w3)
    reduce(1)
    v3p, w3p = arrived(3, moving, [v3, w3])

    gv3 = coarse(v3, v3p)
    gw3 = coarse(w3, w3p)
    finish(3, gw3 + (fine(v3p) - gv3))
    reduce(2)
    reduce(3)
    collect()


def local(initial_state, forcing, w_down, depth_kernel, w_point, w_up):
    tm, spaces, ens = lax.axis_size("tm"), lax.axis_size("space"), lax.axis_size("ens")
    _, fields, half, columns = initial_state.shape
    block = half // tm
    cols, groups = columns // 2, 2 * fields
    layers, ch, _ = depth_kernel.shape
    assert block == FINE == 2 * layers and tm == 4
    assert fields % ens == 0
    count = groups + 2 * forcing.shape[0]
    chunk = fields // ens
    vmem = pl.BlockSpec(memory_space=pltpu.VMEM)
    hbm = pl.BlockSpec(memory_space=pltpu.HBM)
    args = (initial_state, forcing, w_down, depth_kernel, w_point, w_up)
    ending, mean = pl.pallas_call(
        lambda *refs: kernel(tm, spaces, ens, *refs),
        name="parareal",
        out_shape=[jax.ShapeDtypeStruct((fields, half, columns), F32)] * 2,
        in_specs=[hbm] * 6,
        out_specs=[vmem] * 2,
        scratch_shapes=[pltpu.VMEM(a.shape, a.dtype) for a in args] + [
            pltpu.VMEM((3 * block // 2 * ch, groups * 4 * block), BF16),
            pltpu.VMEM((groups * block, block // 2 * ch), BF16),
            pltpu.VMEM((layers, 3 * ch, 3 * ch), BF16),
            pltpu.VMEM((count * block, cols), BF16),
            pltpu.VMEM((count * block, cols), BF16),
            pltpu.VMEM((count * block, cols), BF16),
            pltpu.VMEM((3, 3, groups * block, cols), BF16),
            pltpu.VMEM((3, 3, groups * block, cols), BF16),
            pltpu.VMEM((3, 3, groups * block, cols), BF16),
            pltpu.VMEM((tm, fields, block, columns), F32),
            pltpu.VMEM((tm, max(ens - 1, 1), chunk, block, columns), F32),
            pltpu.VMEM((tm, chunk, block, columns), F32),
            pltpu.VMEM((tm, fields, block, columns), F32),
            pltpu.VMEM((tm, ens, chunk, block, columns), F32),
            pltpu.SemaphoreType.DMA((6,)),
            pltpu.SemaphoreType.DMA((4, 2)),
            pltpu.SemaphoreType.DMA((4, 2)),
            pltpu.SemaphoreType.DMA((tm,)),
            pltpu.SemaphoreType.DMA((tm,)),
            pltpu.SemaphoreType.DMA((tm, max(ens - 1, 1))),
            pltpu.SemaphoreType.DMA((tm, max(ens - 1, 1))),
            pltpu.SemaphoreType.DMA((tm, ens)),
            pltpu.SemaphoreType.DMA((tm, ens)),
        ],
        compiler_params=pltpu.CompilerParams(has_side_effects=True, collective_id=0, vmem_limit_bytes=32 << 20),
    )(*args)
    return ending[None, None], mean[None]


def solution(mesh):
    in_specs = (P("ens", None, "space", None), P(None, "space", None), P(), P(), P(), P())
    out_specs = (P("ens", "tm", None, "space", None), P("tm", None, "space", None))
    return jax.shard_map(local, mesh=mesh, in_specs=in_specs, out_specs=out_specs, check_vma=False)
```

```python
import jax
import jax.numpy as jnp
from jax import lax
from jax.experimental import pallas as pl
from jax.experimental.pallas import tpu as pltpu
from jax.sharding import PartitionSpec as P

TIME_STEP = 0.05
VISCOSITY = 0.5
DIFFUSIVITY = 0.3
FINE = 4
MESH = pl.DeviceIdType.MESH
F32 = jnp.float32
BF16 = jnp.bfloat16


def swap_order(p):
    if isinstance(p, int):
        return p + (p // 2) * (1 - 2 * (p % 2))
    return p + lax.div(p, 2) * (1 - 2 * lax.rem(p, 2))


def iota(shape, dim):
    return lax.broadcasted_iota(jnp.int32, shape, dim)


def split3(x):
    hi = x.astype(BF16)
    rest = x - hi.astype(F32)
    mid = rest.astype(BF16)
    low = (rest - mid.astype(F32)).astype(BF16)
    return jnp.concatenate([hi, mid, low], axis=0)


def exact_move(x, pick):
    rows = x.shape[0]
    y = jnp.dot(split3(x), pick, preferred_element_type=F32)
    return y[:rows] + y[rows : 2 * rows] + y[2 * rows :]


def fine_sweep(state, force):
    cur = state
    rows = cur.shape[1]
    fields = cur.shape[0] // 2
    for _ in range(FINE):
        north = pltpu.roll(cur, 1, 1)
        south = pltpu.roll(cur, rows - 1, 1)
        down = (south - north) * 0.5
        vert = south + north - 4.0 * cur
        out = [None] * (2 * fields)
        for b in (0, 1):
            across, lap = [], []
            for f in range(fields):
                ev, od = cur[2 * f], cur[2 * f + 1]
                cols = ev.shape[1]
                if b == 0:
                    east, west = od, pltpu.roll(od, 1, 1)
                else:
                    east, west = pltpu.roll(ev, cols - 1, 1), ev
                across.append((east - west) * 0.5)
                lap.append(vert[2 * f + b] + east + west)
            u, v = cur[b], cur[2 + b]

            def carried(f):
                return u * across[f] + v * down[2 * f + b]

            rates = [
                VISCOSITY * lap[0] - carried(0) - across[2] + force[b],
                VISCOSITY * lap[1] - carried(1) - down[4 + b] + force[2 + b],
                VISCOSITY * lap[2] - (across[0] + down[2 + b]),
                DIFFUSIVITY * lap[3] - carried(3),
            ]
            for f in range(fields):
                out[2 * f + b] = cur[2 * f + b] + TIME_STEP * rates[f]
        cur = jnp.stack(out)
    return cur


def gelu(x):
    return 0.5 * x * (1.0 + jnp.tanh(0.7978845608028654 * (x + 0.044715 * x * x * x)))


def kernel(tm, spaces, ens, u_hbm, f_hbm, wd_hbm, dk_hbm, wp_hbm, wu_hbm, out_ref, mean_ref,
           u_in, f_in, wd_ref, dk_ref, wp_ref, wu_ref,
           wdb, wub, wcs, snd0, nrt0, sth0, snd, nrt, sth,
           ebuf, parts, mbuf, got, got_mean,
           load_sem, send_sem, recv_sem, end_send, end_recv, part_send, part_recv, mean_send, mean_recv, reach):
    loads = []
    for i, (src, dst) in enumerate([(u_hbm, u_in), (f_hbm, f_in), (wd_hbm, wd_ref), (dk_hbm, dk_ref),
                                    (wp_hbm, wp_ref), (wu_hbm, wu_ref)]):
        loads.append(pltpu.make_async_copy(src, dst, load_sem.at[i]))
    for c in loads:
        c.start()
    u_ref, f_ref = u_in.at[0], f_in
    e = lax.axis_index("ens")
    t = lax.axis_index("tm")
    s = lax.axis_index("space")
    fields, half, columns = u_ref.shape
    cols = columns // 2
    block = half // tm
    ch = wd_ref.shape[0]
    layers = wp_ref.shape[0]
    groups = 2 * fields
    padded = 4 * block
    pos = swap_order(t)
    ring = s * tm + pos
    total = tm * spaces
    neighbours = []
    for step in (total - 1, 1):
        g = lax.rem(ring + step, total)
        neighbours.append({"tm": swap_order(lax.rem(g, tm)), "space": lax.div(g, tm)})
    to_north, to_south = neighbours

    def exchange(stage, src, from_north, from_south):
        copies = [
            pltpu.make_async_remote_copy(src, from_south, send_sem.at[stage, 0], recv_sem.at[stage, 0],
                                         device_id=to_north, device_id_type=MESH),
            pltpu.make_async_remote_copy(src, from_north, send_sem.at[stage, 1], recv_sem.at[stage, 1],
                                         device_id=to_south, device_id_type=MESH),
        ]
        for c in copies:
            c.start()
        return copies

    def own_rows(ref):
        picked = ref[:, 0:block, :]
        for k in range(1, tm):
            picked = jnp.where(pos == k, ref[:, k * block : (k + 1) * block, :], picked)
        return picked

    barrier = pltpu.get_barrier_semaphore()
    same_rows = [{"tm": lax.rem(t + i, tm)} for i in range(1, tm)]
    peers = neighbours + same_rows + [{"ens": lax.rem(e + i, ens)} for i in range(1, ens)]
    for peer in peers:
        pl.semaphore_signal(barrier, inc=1, device_id=peer, device_id_type=MESH)
    loads[0].wait()
    loads[1].wait()
    r_i, c_i = iota((columns, columns), 0), iota((columns, columns), 1)
    odd = jnp.where(c_i >= cols, 1, 0)
    to_parity = jnp.where(r_i == 2 * (c_i - odd * cols) + odd, 1.0, 0.0).astype(BF16)
    both = jnp.concatenate([own_rows(u_ref), own_rows(f_ref)], axis=0)
    count = fields + f_ref.shape[0]
    moved = exact_move(both.reshape(count * block, columns), to_parity).reshape(count, block, columns)
    first = []
    for f in range(count):
        for b in (0, 1):
            first.append(moved[f, :, b * cols : (b + 1) * cols])
    first = jnp.stack(first)
    snd0[...] = first.reshape(2 * count * block, cols).astype(snd0.dtype)
    pl.semaphore_wait(barrier, len(peers))
    for peer in same_rows:
        pl.semaphore_signal(reach, inc=1, device_id=peer, device_id_type=MESH)
    copies = exchange(0, snd0, nrt0, sth0)

    for c in loads[2:]:
        c.wait()
    rows_in = 3 * block // 2
    wide = groups * padded
    for r in range(rows_in):
        q, k = iota((2 * groups, wide), 0), iota((2 * groups, wide), 1)
        fq, aq, bq = q // 4, (q // 2) % 2, q % 2
        gk, rk = k // padded, k % padded
        sel = jnp.where((gk == 2 * fq + bq) & (rk == 2 * r + aq), 1.0, 0.0).astype(BF16)
        wdb[r * ch : (r + 1) * ch] = jnp.dot(wd_ref[...], sel, preferred_element_type=F32).astype(BF16)
    small = groups * block
    for r in range(block // 2):
        q, k = iota((small, 2 * groups), 1), iota((small, 2 * groups), 0)
        fq, aq, bq = q // 4, (q // 2) % 2, q % 2
        gk, rk = k // block, k % block
        sel = jnp.where((gk == 2 * fq + bq) & (rk == 2 * r + aq), 1.0, 0.0).astype(BF16)
        wub[:, r * ch : (r + 1) * ch] = jnp.dot(sel, wu_ref[...], preferred_element_type=F32).astype(BF16)
    for l in range(layers):
        w = wp_ref[l].astype(F32)
        taps = dk_ref[l].T
        for a in range(3):
            for b in range(3):
                tap = taps[3 * a + b : 3 * a + b + 1, :]
                wcs[l, b * ch : (b + 1) * ch, a * ch : (a + 1) * ch] = (w * tap).astype(BF16)

    def coarse(own, state):
        x = state.astype(BF16).reshape(wide, cols)
        hidden = jnp.dot(wdb[...], x, preferred_element_type=F32).astype(BF16)
        for l in range(layers):
            n_out = hidden.shape[0] // ch - 2
            new = []
            for r in range(n_out):
                y = jnp.dot(wcs[l], hidden[r * ch : (r + 3) * ch], preferred_element_type=F32)
                lifted = y[ch : 2 * ch] + pltpu.roll(y[:ch], 1, 1) + pltpu.roll(y[2 * ch :], cols - 1, 1)
                old = hidden[(r + 1) * ch : (r + 2) * ch].astype(F32)
                new.append((old + gelu(lifted)).astype(BF16))
            hidden = jnp.concatenate(new, axis=0)
        delta = jnp.dot(wub[...], hidden, preferred_element_type=F32)
        return own + delta.reshape(groups, block, cols)

    def fine(state):
        return fine_sweep(state, force)[:, block : 2 * block]

    def unpack(x):
        return x.astype(F32).reshape(-1, block, cols)

    def pad(north, own, south):
        return jnp.concatenate([north, own, south, jnp.zeros_like(own)], axis=1)

    r_j, c_j = iota((columns, columns), 0), iota((columns, columns), 1)
    odd_j = jnp.where(r_j >= cols, 1, 0)
    from_parity = jnp.where(c_j == 2 * (r_j - odd_j * cols) + odd_j, 1.0, 0.0).astype(BF16)

    chunk = fields // ens

    def finish(n, end):
        pieces = [jnp.concatenate([end[2 * f], end[2 * f + 1]], axis=1) for f in range(fields)]
        flat = jnp.concatenate(pieces, axis=0)
        ebuf[n] = exact_move(flat, from_parity).reshape(fields, block, columns)
        for d in range(1, ens):
            part_copy(n, d).start()

        @pl.when(t != n)
        def _():
            end_copy(n).start()

    def part_copy(n, d):
        other = lax.rem(e + d, ens)
        return pltpu.make_async_remote_copy(
            ebuf.at[n, pl.ds(other * chunk, chunk)], parts.at[n, d - 1], part_send.at[n, d - 1], part_recv.at[n, d - 1],
            device_id={"ens": other}, device_id_type=MESH)

    def end_copy(n):
        return pltpu.make_async_remote_copy(
            ebuf.at[n], got.at[pos], end_send.at[n], end_recv.at[t],
            device_id={"tm": n}, device_id_type=MESH)

    def mean_copy(n, d):
        return pltpu.make_async_remote_copy(
            mbuf.at[n], got_mean.at[pos, d], mean_send.at[n, d], mean_recv.at[t, d],
            device_id={"tm": n, "ens": lax.rem(e + d, ens)}, device_id_type=MESH)

    def reduce(n):
        acc = ebuf[n, pl.ds(e * chunk, chunk)]
        for d in range(1, ens):
            part_copy(n, d).wait()
            acc = acc + parts[n, d - 1]
        mbuf[n] = acc * (1.0 / ens)
        for d in range(1, ens):
            mean_copy(n, d).start()

        @pl.when(t != n)
        def _():
            mean_copy(n, 0).start()

    def collect():
        for n in range(tm):
            @pl.when(t != n)
            def _():
                end_copy(n).wait_send()
                mean_copy(n, 0).wait_send()
                pltpu.make_async_remote_copy(
                    ebuf.at[n], got.at[swap_order(n)], end_send.at[n], end_recv.at[n],
                    device_id={"tm": n}, device_id_type=MESH).wait_recv()
                pltpu.make_async_remote_copy(
                    mbuf.at[n], got_mean.at[swap_order(n), 0], mean_send.at[n, 0], mean_recv.at[n, 0],
                    device_id={"tm": n}, device_id_type=MESH).wait_recv()

            @pl.when(t == n)
            def _():
                got[swap_order(n)] = ebuf[n]
                got_mean[swap_order(n), 0] = mbuf[n]

            for d in range(1, ens):
                mean_copy(n, d).wait_send()
                pltpu.make_async_remote_copy(
                    mbuf.at[n], got_mean.at[swap_order(n), d], mean_send.at[n, d], mean_recv.at[n, d],
                    device_id={"ens": lax.rem(e + d, ens)}, device_id_type=MESH).wait_recv()
        for p in range(tm):
            out_ref[:, p * block : (p + 1) * block, :] = got[p]
            for d in range(ens):
                first = lax.rem(e + ens - d, ens) * chunk
                mean_ref[pl.ds(first, chunk), p * block : (p + 1) * block, :] = got_mean[p, d]

    def next_stage(stage, starts):
        for i, start in enumerate(starts):
            snd[stage - 1, i] = start.reshape(groups * block, cols).astype(snd.dtype)
        k = len(starts)
        return exchange(stage, snd.at[stage - 1, 0:k], nrt.at[stage - 1, 0:k], sth.at[stage - 1, 0:k])

    def arrived(stage, moving, starts):
        for c in moving:
            c.wait()
        return [pad(unpack(nrt[stage - 1, i]), start, unpack(sth[stage - 1, i])) for i, start in enumerate(starts)]

    for c in copies:
        c.wait()
    everything = pad(unpack(nrt0[...]), first, unpack(sth0[...]))
    force = everything[groups:]
    start0 = first[:groups]
    state0 = everything[:groups]

    g0 = coarse(start0, state0)
    v1 = g0 + (fine(state0) - g0)
    u1 = g0
    moving = next_stage(1, [u1, v1])
    finish(0, v1)
    u1p, v1p = arrived(1, moving, [u1, v1])

    u2 = coarse(u1, u1p)
    gv1 = coarse(v1, v1p)
    v2 = gv1 + (fine(u1p) - u2)
    w2 = gv1 + (fine(v1p) - gv1)
    moving = next_stage(2, [u2, v2, w2])
    finish(1, w2)
    pl.semaphore_wait(reach, len(same_rows))
    reduce(0)
    u2p, v2p, w2p = arrived(2, moving, [u2, v2, w2])

    gu2 = coarse(u2, u2p)
    gv2 = coarse(v2, v2p)
    gw2 = coarse(w2, w2p)
    v3 = gv2 + (fine(u2p) - gu2)
    w3 = gw2 + (fine(v2p) - gv2)
    moving = next_stage(3, [v3, w3])
    finish(2, w3)
    reduce(1)
    v3p, w3p = arrived(3, moving, [v3, w3])

    gv3 = coarse(v3, v3p)
    gw3 = coarse(w3, w3p)
    finish(3, gw3 + (fine(v3p) - gv3))
    reduce(2)
    reduce(3)
    collect()


def local(initial_state, forcing, w_down, depth_kernel, w_point, w_up):
    tm, spaces, ens = lax.axis_size("tm"), lax.axis_size("space"), lax.axis_size("ens")
    _, fields, half, columns = initial_state.shape
    block = half // tm
    cols, groups = columns // 2, 2 * fields
    layers, ch, _ = depth_kernel.shape
    assert block == FINE == 2 * layers and tm == 4
    assert fields % ens == 0
    count = groups + 2 * forcing.shape[0]
    chunk = fields // ens
    vmem = pl.BlockSpec(memory_space=pltpu.VMEM)
    hbm = pl.BlockSpec(memory_space=pltpu.HBM)
    args = (initial_state, forcing, w_down, depth_kernel, w_point, w_up)
    ending, mean = pl.pallas_call(
        lambda *refs: kernel(tm, spaces, ens, *refs),
        name="parareal",
        out_shape=[jax.ShapeDtypeStruct((fields, half, columns), F32)] * 2,
        in_specs=[hbm] * 6,
        out_specs=[vmem] * 2,
        scratch_shapes=[pltpu.VMEM(a.shape, a.dtype) for a in args] + [
            pltpu.VMEM((3 * block // 2 * ch, groups * 4 * block), BF16),
            pltpu.VMEM((groups * block, block // 2 * ch), BF16),
            pltpu.VMEM((layers, 3 * ch, 3 * ch), BF16),
            pltpu.VMEM((count * block, cols), BF16),
            pltpu.VMEM((count * block, cols), BF16),
            pltpu.VMEM((count * block, cols), BF16),
            pltpu.VMEM((3, 3, groups * block, cols), BF16),
            pltpu.VMEM((3, 3, groups * block, cols), BF16),
            pltpu.VMEM((3, 3, groups * block, cols), BF16),
            pltpu.VMEM((tm, fields, block, columns), F32),
            pltpu.VMEM((tm, max(ens - 1, 1), chunk, block, columns), F32),
            pltpu.VMEM((tm, chunk, block, columns), F32),
            pltpu.VMEM((tm, fields, block, columns), F32),
            pltpu.VMEM((tm, ens, chunk, block, columns), F32),
            pltpu.SemaphoreType.DMA((6,)),
            pltpu.SemaphoreType.DMA((4, 2)),
            pltpu.SemaphoreType.DMA((4, 2)),
            pltpu.SemaphoreType.DMA((tm,)),
            pltpu.SemaphoreType.DMA((tm,)),
            pltpu.SemaphoreType.DMA((tm, max(ens - 1, 1))),
            pltpu.SemaphoreType.DMA((tm, max(ens - 1, 1))),
            pltpu.SemaphoreType.DMA((tm, ens)),
            pltpu.SemaphoreType.DMA((tm, ens)),
            pltpu.SemaphoreType.REGULAR,
        ],
        compiler_params=pltpu.CompilerParams(has_side_effects=True, collective_id=0, vmem_limit_bytes=32 << 20),
    )(*args)
    return ending[None, None], mean[None]


def solution(mesh):
    in_specs = (P("ens", None, "space", None), P(None, "space", None), P(), P(), P(), P())
    out_specs = (P("ens", "tm", None, "space", None), P("tm", None, "space", None))
    return jax.shard_map(local, mesh=mesh, in_specs=in_specs, out_specs=out_specs, check_vma=False)
```

```python
import jax
import jax.numpy as jnp
from jax import lax
from jax.experimental import pallas as pl
from jax.experimental.pallas import tpu as pltpu
from jax.sharding import PartitionSpec as P

TIME_STEP = 0.05
VISCOSITY = 0.5
DIFFUSIVITY = 0.3
FINE = 4
MESH = pl.DeviceIdType.MESH
F32 = jnp.float32
BF16 = jnp.bfloat16


def swap_order(p):
    if isinstance(p, int):
        return p + (p // 2) * (1 - 2 * (p % 2))
    return p + lax.div(p, 2) * (1 - 2 * lax.rem(p, 2))


def iota(shape, dim):
    return lax.broadcasted_iota(jnp.int32, shape, dim)


def split3(x):
    hi = x.astype(BF16)
    rest = x - hi.astype(F32)
    mid = rest.astype(BF16)
    low = (rest - mid.astype(F32)).astype(BF16)
    return jnp.concatenate([hi, mid, low], axis=0)


def exact_move(x, pick):
    rows = x.shape[0]
    y = jnp.dot(split3(x), pick, preferred_element_type=F32)
    return y[:rows] + y[rows : 2 * rows] + y[2 * rows :]


def fine_sweep(state, force):
    cur = state
    rows = cur.shape[1]
    fields = cur.shape[0] // 2
    for _ in range(FINE):
        north = pltpu.roll(cur, 1, 1)
        south = pltpu.roll(cur, rows - 1, 1)
        down = (south - north) * 0.5
        vert = south + north - 4.0 * cur
        out = [None] * (2 * fields)
        for b in (0, 1):
            across, lap = [], []
            for f in range(fields):
                ev, od = cur[2 * f], cur[2 * f + 1]
                cols = ev.shape[1]
                if b == 0:
                    east, west = od, pltpu.roll(od, 1, 1)
                else:
                    east, west = pltpu.roll(ev, cols - 1, 1), ev
                across.append((east - west) * 0.5)
                lap.append(vert[2 * f + b] + east + west)
            u, v = cur[b], cur[2 + b]

            def carried(f):
                return u * across[f] + v * down[2 * f + b]

            rates = [
                VISCOSITY * lap[0] - carried(0) - across[2] + force[b],
                VISCOSITY * lap[1] - carried(1) - down[4 + b] + force[2 + b],
                VISCOSITY * lap[2] - (across[0] + down[2 + b]),
                DIFFUSIVITY * lap[3] - carried(3),
            ]
            for f in range(fields):
                out[2 * f + b] = cur[2 * f + b] + TIME_STEP * rates[f]
        cur = jnp.stack(out)
    return cur


def gelu(x):
    return 0.5 * x * (1.0 + jnp.tanh(0.7978845608028654 * (x + 0.044715 * x * x * x)))


def kernel(tm, spaces, ens, u_hbm, f_hbm, wd_hbm, dk_hbm, wp_hbm, wu_hbm, out_ref, mean_ref,
           u_in, f_in, wd_ref, dk_ref, wp_ref, wu_ref,
           wdb, wub, wcs, snd0, nrt0, sth0, snd, nrt, sth,
           ebuf, parts, mbuf, got, got_mean,
           load_sem, send_sem, recv_sem, end_send, end_recv, part_send, part_recv, mean_send, mean_recv, reach):
    loads = []
    for i, (src, dst) in enumerate([(u_hbm, u_in), (f_hbm, f_in), (wd_hbm, wd_ref), (dk_hbm, dk_ref),
                                    (wp_hbm, wp_ref), (wu_hbm, wu_ref)]):
        loads.append(pltpu.make_async_copy(src, dst, load_sem.at[i]))
    for c in loads:
        c.start()
    u_ref, f_ref = u_in.at[0], f_in
    e = lax.axis_index("ens")
    t = lax.axis_index("tm")
    s = lax.axis_index("space")
    fields, half, columns = u_ref.shape
    cols = columns // 2
    block = half // tm
    ch = wd_ref.shape[0]
    layers = wp_ref.shape[0]
    groups = 2 * fields
    padded = 4 * block
    pos = swap_order(t)
    ring = s * tm + pos
    total = tm * spaces
    neighbours = []
    for step in (total - 1, 1):
        g = lax.rem(ring + step, total)
        neighbours.append({"tm": swap_order(lax.rem(g, tm)), "space": lax.div(g, tm)})
    to_north, to_south = neighbours

    def exchange(stage, src, from_north, from_south):
        copies = [
            pltpu.make_async_remote_copy(src, from_south, send_sem.at[stage, 0], recv_sem.at[stage, 0],
                                         device_id=to_north, device_id_type=MESH),
            pltpu.make_async_remote_copy(src, from_north, send_sem.at[stage, 1], recv_sem.at[stage, 1],
                                         device_id=to_south, device_id_type=MESH),
        ]
        for c in copies:
            c.start()
        return copies

    def own_rows(ref):
        picked = ref[:, 0:block, :]
        for k in range(1, tm):
            picked = jnp.where(pos == k, ref[:, k * block : (k + 1) * block, :], picked)
        return picked

    barrier = pltpu.get_barrier_semaphore()
    same_rows = [{"tm": lax.rem(t + i, tm)} for i in range(1, tm)]
    peers = same_rows + [{"ens": lax.rem(e + i, ens)} for i in range(1, ens)]
    for peer in peers:
        pl.semaphore_signal(barrier, inc=1, device_id=peer, device_id_type=MESH)
    for edge, across in ((0, to_north), (tm - 1, to_south)):
        @pl.when(pos == edge)
        def _():
            pl.semaphore_signal(barrier, inc=1, device_id=across, device_id_type=MESH)
    loads[0].wait()
    loads[1].wait()
    r_i, c_i = iota((columns, columns), 0), iota((columns, columns), 1)
    odd = jnp.where(c_i >= cols, 1, 0)
    to_parity = jnp.where(r_i == 2 * (c_i - odd * cols) + odd, 1.0, 0.0).astype(BF16)
    both = jnp.concatenate([own_rows(u_ref), own_rows(f_ref)], axis=0)
    count = fields + f_ref.shape[0]
    moved = exact_move(both.reshape(count * block, columns), to_parity).reshape(count, block, columns)
    first = []
    for f in range(count):
        for b in (0, 1):
            first.append(moved[f, :, b * cols : (b + 1) * cols])
    first = jnp.stack(first)
    snd0[...] = first.reshape(2 * count * block, cols).astype(snd0.dtype)
    pl.semaphore_wait(barrier, len(peers) + jnp.where((pos == 0) | (pos == tm - 1), 1, 0))
    for peer in same_rows:
        pl.semaphore_signal(reach, inc=1, device_id=peer, device_id_type=MESH)
    copies = exchange(0, snd0, nrt0, sth0)

    for c in loads[2:]:
        c.wait()
    rows_in = 3 * block // 2
    wide = groups * padded
    for r in range(rows_in):
        q, k = iota((2 * groups, wide), 0), iota((2 * groups, wide), 1)
        fq, aq, bq = q // 4, (q // 2) % 2, q % 2
        gk, rk = k // padded, k % padded
        sel = jnp.where((gk == 2 * fq + bq) & (rk == 2 * r + aq), 1.0, 0.0).astype(BF16)
        wdb[r * ch : (r + 1) * ch] = jnp.dot(wd_ref[...], sel, preferred_element_type=F32).astype(BF16)
    small = groups * block
    for r in range(block // 2):
        q, k = iota((small, 2 * groups), 1), iota((small, 2 * groups), 0)
        fq, aq, bq = q // 4, (q // 2) % 2, q % 2
        gk, rk = k // block, k % block
        sel = jnp.where((gk == 2 * fq + bq) & (rk == 2 * r + aq), 1.0, 0.0).astype(BF16)
        wub[:, r * ch : (r + 1) * ch] = jnp.dot(sel, wu_ref[...], preferred_element_type=F32).astype(BF16)
    for l in range(layers):
        w = wp_ref[l].astype(F32)
        taps = dk_ref[l].T
        for a in range(3):
            for b in range(3):
                tap = taps[3 * a + b : 3 * a + b + 1, :]
                wcs[l, b * ch : (b + 1) * ch, a * ch : (a + 1) * ch] = (w * tap).astype(BF16)

    def coarse(own, state):
        x = state.astype(BF16).reshape(wide, cols)
        hidden = jnp.dot(wdb[...], x, preferred_element_type=F32).astype(BF16)
        for l in range(layers):
            n_out = hidden.shape[0] // ch - 2
            new = []
            for r in range(n_out):
                y = jnp.dot(wcs[l], hidden[r * ch : (r + 3) * ch], preferred_element_type=F32)
                lifted = y[ch : 2 * ch] + pltpu.roll(y[:ch], 1, 1) + pltpu.roll(y[2 * ch :], cols - 1, 1)
                old = hidden[(r + 1) * ch : (r + 2) * ch].astype(F32)
                new.append((old + gelu(lifted)).astype(BF16))
            hidden = jnp.concatenate(new, axis=0)
        delta = jnp.dot(wub[...], hidden, preferred_element_type=F32)
        return own + delta.reshape(groups, block, cols)

    def fine(state):
        return fine_sweep(state, force)[:, block : 2 * block]

    def unpack(x):
        return x.astype(F32).reshape(-1, block, cols)

    def pad(north, own, south):
        return jnp.concatenate([north, own, south, jnp.zeros_like(own)], axis=1)

    r_j, c_j = iota((columns, columns), 0), iota((columns, columns), 1)
    odd_j = jnp.where(r_j >= cols, 1, 0)
    from_parity = jnp.where(c_j == 2 * (r_j - odd_j * cols) + odd_j, 1.0, 0.0).astype(BF16)

    chunk = fields // ens

    def finish(n, end):
        pieces = [jnp.concatenate([end[2 * f], end[2 * f + 1]], axis=1) for f in range(fields)]
        flat = jnp.concatenate(pieces, axis=0)
        ebuf[n] = exact_move(flat, from_parity).reshape(fields, block, columns)
        for d in range(1, ens):
            part_copy(n, d).start()

        @pl.when(t != n)
        def _():
            end_copy(n).start()

    def part_copy(n, d):
        other = lax.rem(e + d, ens)
        return pltpu.make_async_remote_copy(
            ebuf.at[n, pl.ds(other * chunk, chunk)], parts.at[n, d - 1], part_send.at[n, d - 1], part_recv.at[n, d - 1],
            device_id={"ens": other}, device_id_type=MESH)

    def end_copy(n):
        return pltpu.make_async_remote_copy(
            ebuf.at[n], got.at[pos], end_send.at[n], end_recv.at[t],
            device_id={"tm": n}, device_id_type=MESH)

    def mean_copy(n, d):
        return pltpu.make_async_remote_copy(
            mbuf.at[n], got_mean.at[pos, d], mean_send.at[n, d], mean_recv.at[t, d],
            device_id={"tm": n, "ens": lax.rem(e + d, ens)}, device_id_type=MESH)

    def reduce(n):
        acc = ebuf[n, pl.ds(e * chunk, chunk)]
        for d in range(1, ens):
            part_copy(n, d).wait()
            acc = acc + parts[n, d - 1]
        mbuf[n] = acc * (1.0 / ens)
        for d in range(1, ens):
            mean_copy(n, d).start()

        @pl.when(t != n)
        def _():
            mean_copy(n, 0).start()

    def collect():
        for n in range(tm):
            @pl.when(t != n)
            def _():
                end_copy(n).wait_send()
                mean_copy(n, 0).wait_send()
                pltpu.make_async_remote_copy(
                    ebuf.at[n], got.at[swap_order(n)], end_send.at[n], end_recv.at[n],
                    device_id={"tm": n}, device_id_type=MESH).wait_recv()
                pltpu.make_async_remote_copy(
                    mbuf.at[n], got_mean.at[swap_order(n), 0], mean_send.at[n, 0], mean_recv.at[n, 0],
                    device_id={"tm": n}, device_id_type=MESH).wait_recv()

            @pl.when(t == n)
            def _():
                got[swap_order(n)] = ebuf[n]
                got_mean[swap_order(n), 0] = mbuf[n]

            for d in range(1, ens):
                mean_copy(n, d).wait_send()
                pltpu.make_async_remote_copy(
                    mbuf.at[n], got_mean.at[swap_order(n), d], mean_send.at[n, d], mean_recv.at[n, d],
                    device_id={"ens": lax.rem(e + d, ens)}, device_id_type=MESH).wait_recv()
        for p in range(tm):
            out_ref[:, p * block : (p + 1) * block, :] = got[p]
            for d in range(ens):
                first = lax.rem(e + ens - d, ens) * chunk
                mean_ref[pl.ds(first, chunk), p * block : (p + 1) * block, :] = got_mean[p, d]

    def next_stage(stage, starts):
        for i, start in enumerate(starts):
            snd[stage - 1, i] = start.reshape(groups * block, cols).astype(snd.dtype)
        k = len(starts)
        return exchange(stage, snd.at[stage - 1, 0:k], nrt.at[stage - 1, 0:k], sth.at[stage - 1, 0:k])

    def arrived(stage, moving, starts):
        for c in moving:
            c.wait()
        return [pad(unpack(nrt[stage - 1, i]), start, unpack(sth[stage - 1, i])) for i, start in enumerate(starts)]

    for c in copies:
        c.wait()
    everything = pad(unpack(nrt0[...]), first, unpack(sth0[...]))
    force = everything[groups:]
    start0 = first[:groups]
    state0 = everything[:groups]

    g0 = coarse(start0, state0)
    v1 = g0 + (fine(state0) - g0)
    u1 = g0
    moving = next_stage(1, [u1, v1])
    finish(0, v1)
    u1p, v1p = arrived(1, moving, [u1, v1])

    u2 = coarse(u1, u1p)
    gv1 = coarse(v1, v1p)
    v2 = gv1 + (fine(u1p) - u2)
    w2 = gv1 + (fine(v1p) - gv1)
    moving = next_stage(2, [u2, v2, w2])
    finish(1, w2)
    pl.semaphore_wait(reach, len(same_rows))
    reduce(0)
    u2p, v2p, w2p = arrived(2, moving, [u2, v2, w2])

    gu2 = coarse(u2, u2p)
    gv2 = coarse(v2, v2p)
    gw2 = coarse(w2, w2p)
    v3 = gv2 + (fine(u2p) - gu2)
    w3 = gw2 + (fine(v2p) - gv2)
    moving = next_stage(3, [v3, w3])
    finish(2, w3)
    reduce(1)
    v3p, w3p = arrived(3, moving, [v3, w3])

    gv3 = coarse(v3, v3p)
    gw3 = coarse(w3, w3p)
    finish(3, gw3 + (fine(v3p) - gv3))
    reduce(2)
    reduce(3)
    collect()


def local(initial_state, forcing, w_down, depth_kernel, w_point, w_up):
    tm, spaces, ens = lax.axis_size("tm"), lax.axis_size("space"), lax.axis_size("ens")
    _, fields, half, columns = initial_state.shape
    block = half // tm
    cols, groups = columns // 2, 2 * fields
    layers, ch, _ = depth_kernel.shape
    assert block == FINE == 2 * layers and tm == 4
    assert fields % ens == 0
    count = groups + 2 * forcing.shape[0]
    chunk = fields // ens
    vmem = pl.BlockSpec(memory_space=pltpu.VMEM)
    hbm = pl.BlockSpec(memory_space=pltpu.HBM)
    args = (initial_state, forcing, w_down, depth_kernel, w_point, w_up)
    ending, mean = pl.pallas_call(
        lambda *refs: kernel(tm, spaces, ens, *refs),
        name="parareal",
        out_shape=[jax.ShapeDtypeStruct((fields, half, columns), F32)] * 2,
        in_specs=[hbm] * 6,
        out_specs=[vmem] * 2,
        scratch_shapes=[pltpu.VMEM(a.shape, a.dtype) for a in args] + [
            pltpu.VMEM((3 * block // 2 * ch, groups * 4 * block), BF16),
            pltpu.VMEM((groups * block, block // 2 * ch), BF16),
            pltpu.VMEM((layers, 3 * ch, 3 * ch), BF16),
            pltpu.VMEM((count * block, cols), BF16),
            pltpu.VMEM((count * block, cols), BF16),
            pltpu.VMEM((count * block, cols), BF16),
            pltpu.VMEM((3, 3, groups * block, cols), BF16),
            pltpu.VMEM((3, 3, groups * block, cols), BF16),
            pltpu.VMEM((3, 3, groups * block, cols), BF16),
            pltpu.VMEM((tm, fields, block, columns), F32),
            pltpu.VMEM((tm, max(ens - 1, 1), chunk, block, columns), F32),
            pltpu.VMEM((tm, chunk, block, columns), F32),
            pltpu.VMEM((tm, fields, block, columns), F32),
            pltpu.VMEM((tm, ens, chunk, block, columns), F32),
            pltpu.SemaphoreType.DMA((6,)),
            pltpu.SemaphoreType.DMA((4, 2)),
            pltpu.SemaphoreType.DMA((4, 2)),
            pltpu.SemaphoreType.DMA((tm,)),
            pltpu.SemaphoreType.DMA((tm,)),
            pltpu.SemaphoreType.DMA((tm, max(ens - 1, 1))),
            pltpu.SemaphoreType.DMA((tm, max(ens - 1, 1))),
            pltpu.SemaphoreType.DMA((tm, ens)),
            pltpu.SemaphoreType.DMA((tm, ens)),
            pltpu.SemaphoreType.REGULAR,
        ],
        compiler_params=pltpu.CompilerParams(has_side_effects=True, collective_id=0, vmem_limit_bytes=32 << 20),
    )(*args)
    return ending[None, None], mean[None]


def solution(mesh):
    in_specs = (P("ens", None, "space", None), P(None, "space", None), P(), P(), P(), P())
    out_specs = (P("ens", "tm", None, "space", None), P("tm", None, "space", None))
    return jax.shard_map(local, mesh=mesh, in_specs=in_specs, out_specs=out_specs, check_vma=False)
```
